32 devices in a mesh: img: 4 (over x, core), pos: 8 (over z, y).
Axes of the slice: x: 2, y: 2, z: 4, core: 2. Of those that a mesh axis runs over, the one named last changes fastest.
Arguments:
- features: bfloat16 [4096, 16, 1536], P(('img', 'pos')), may hold values from -6 to 6
- channel_index: int32 [550], replicated, may hold values from 0 to 1535, as said below
- image_counts: int32 [32], P(('img', 'pos')), may hold values from 32 to 128, as said below
Outputs:
- centres: float32 [16, 550], P('pos')
- covars: float32 [16, 550, 550], P('pos')
The draws below stay inside these ranges and needn't reach their ends.
Inputs may be any that keep to these rules, and one draw needn't show every extreme that they name: `channel_index`: distinct channel numbers. `image_counts`: some device uses all 128 slots and some only a quarter.
All inputs are finite; a program needn't handle non-finite values.
Results may differ from the reference program's by a relative error of at most 0.0003.
Values may be sent and summed in bfloat16 or wider, within the bound.
No kernel may reach another device: no remote copies, remote signals or barrier semaphores. Data moves between devices by JAX's collectives and lax.ppermute only.
A program may use at most 128 MiB of HBM per device.

```python
import jax
import jax.numpy as jnp
from jax import lax

C_IN = 1536
K = 550
IMG_DEV = 128
POS = 16
IMAGES = 4096
DEVICES = 32


def draw_channel_index(key, part):
    return jax.random.permutation(jax.random.fold_in(key, 11), C_IN)[:K].astype(jnp.int32)


def draw_image_counts(key, part):
    key_vals = jax.random.fold_in(key, 21)
    key_perm = jax.random.fold_in(key, 22)
    values = jax.random.randint(key_vals, (DEVICES,), IMG_DEV // 4, IMG_DEV + 1).astype(jnp.int32)
    order = jax.random.permutation(key_perm, DEVICES)
    values = values.at[order[0]].set(IMG_DEV)
    values = values.at[order[1]].set(IMG_DEV // 4)
    return values


def shard_levels(key, extent, split, smallest, largest):
    loudness = 1.0
    for dim, shards_of in split:
        draws = jax.random.uniform(jax.random.fold_in(jax.random.fold_in(key, 6), dim), (shards_of,), jnp.float32, smallest / len(split), largest / len(split))
        loudness = loudness * jnp.repeat(jnp.exp(draws), extent[dim] // shards_of).reshape((-1,) + (1,) * (len(extent) - 1 - dim))
    return loudness


def bell_draw(key, extent, width, reach, pieces=(), kind=jnp.bfloat16):
    result = width * jax.random.normal(key, extent, jnp.float32)
    if pieces:
        result = result * shard_levels(key, extent, pieces, -0.22, 0.18)
    return jnp.clip(result, -reach, reach).astype(kind)


def setup_inputs(seed: int = 0) -> dict:
    seeds = jax.random.split(jax.random.key(seed), 4)
    return {
        "features": bell_draw(seeds[0], (IMAGES, POS, C_IN), 1.0, 6.0, ((0, 32),)),
        "channel_index": draw_channel_index(jax.random.fold_in(seeds[3], 71), 0),
        "image_counts": draw_image_counts(jax.random.fold_in(seeds[3], 71), 0),
    }


REG = 0.01


def reference(features, channel_index, image_counts):
    images = features.shape[0]
    slot_index = jnp.arange(images, dtype=jnp.int32)
    usable = (slot_index % IMG_DEV) < image_counts[slot_index // IMG_DEV]
    weight_row = usable.astype(jnp.float32)
    total_count = jnp.sum(image_counts.astype(jnp.float32))
    identity_mat = jnp.eye(K, dtype=jnp.float32)

    def one_position(position):
        at_position = lax.dynamic_index_in_dim(features, position, 1, keepdims=False)
        chosen = jnp.take(at_position, channel_index, axis=1).astype(jnp.float32) * weight_row[:, None]
        sq_sum = jnp.dot(chosen.T, chosen, precision=lax.Precision.HIGHEST)
        lin_sum = jnp.sum(chosen, axis=0)
        centre = lin_sum / total_count
        scatter_mat = sq_sum - total_count * jnp.outer(centre, centre)
        return centre, scatter_mat / (total_count - 1.0) + REG * identity_mat

    centres, covars = lax.map(one_position, jnp.arange(POS, dtype=jnp.int32))
    return centres, covars
```

```python
import functools

import jax
import jax.numpy as jnp
from jax import lax
from jax.experimental import pallas as pl
from jax.experimental.pallas import tpu as pltpu
from jax.sharding import PartitionSpec as P

REG = 0.01
LANES = 128
CORES = 2
AXES = ("img", "pos")


def ceil_to(n, m):
    return -(-n // m) * m


class Plan:
    def __init__(self, mesh, slots, positions, width):
        images, owners = mesh.shape["img"], mesh.shape["pos"]
        self.x = images // CORES
        self.y = 1
        while (self.y * 2) ** 2 <= owners and owners % (self.y * 2) == 0:
            self.y *= 2
        self.z = owners // self.y
        self.owners = owners
        self.slots, self.positions, self.width = slots, positions, width
        assert images % CORES == 0 and positions == owners * CORES
        self.blocks = (width + 1) // LANES
        self.main = self.blocks * LANES
        self.tail = width + 1 - self.main
        assert self.tail <= LANES // 2 and self.y % 2 == 0
        self.tail8 = ceil_to(self.tail, 8)
        pairs = [(i, j) for i in range(self.blocks) for j in range(i + 1, self.blocks)]
        self.row_of = {}
        at = 0
        for pair in pairs:
            self.row_of[pair] = at
            at += LANES
        for i in range(0, self.blocks, 2):
            self.row_of[(i, i)] = at
            at += LANES
        for j in range(self.blocks + 1):
            self.row_of[("tail", j)] = at
            at += self.tail8
        self.row_of["diag"] = at
        self.rows = at + ceil_to(-(-self.blocks // 2), 8)

    def moved(self, dx=0, dc=0, dz=0, dy=0):
        pairs = []
        for x in range(self.x):
            for c in range(CORES):
                for z in range(self.z):
                    for y in range(self.y):
                        to = (
                            ((x + dx) % self.x * CORES + (c + dc) % CORES) * self.owners
                            + (z + dz) % self.z * self.y
                            + (y + dy) % self.y
                        )
                        here = (x * CORES + c) * self.owners + z * self.y + y
                        pairs.append((here, to))
        return pairs

    def send(self, value, **step):
        if all(v == 0 for v in step.values()):
            return value
        return lax.ppermute(value, AXES, self.moved(**step))


def select_kernel(plan, block, place_ref, index_ref, x_ref, *refs):
    outs, (onehot, picked) = refs[:-2], refs[-2:]
    step = pl.program_id(0)
    channels = x_ref.shape[2]
    main, tail, padded = plan.main, plan.tail, plan.main + LANES

    @pl.when(step == 0)
    def _():
        rows = lax.broadcasted_iota(jnp.int32, (channels, LANES), 0)
        for j in range(plan.blocks):
            at = slice(j * LANES, (j + 1) * LANES)
            onehot[:, at] = jnp.where(rows == index_ref[:, at], 1.0, 0.0).astype(jnp.bfloat16)
        last = index_ref[:, main : plan.width]
        half = jnp.concatenate([last, jnp.full((1, LANES // 2 - last.shape[1]), -1, jnp.int32)], axis=1)
        both = jnp.concatenate([half, half], axis=1)
        onehot[:, main:padded] = jnp.where(rows == both, 1.0, 0.0).astype(jnp.bfloat16)

    x = x_ref[...].reshape(block * plan.positions, channels)
    got = jnp.dot(x, onehot[...], preferred_element_type=jnp.float32)
    image = step * block + lax.broadcasted_iota(jnp.int32, (block * plan.positions, 1), 0) // plan.positions
    used = image < place_ref[3]
    lane = lax.broadcasted_iota(jnp.int32, (1, padded), 1)
    ones = (lane == main + tail - 1) | (lane == main + LANES // 2 + tail - 1)
    got = jnp.where(used, jnp.where(ones, 1.0, got), 0.0)
    for j in range(plan.blocks + 1):
        picked[j] = got[:, j * LANES : (j + 1) * LANES]
    at = 0
    left = lax.broadcasted_iota(jnp.int32, (1, LANES), 1) < LANES // 2
    for dz in range(plan.z):
        for dc in range(CORES):
            tails = []
            for dy in range(plan.y):
                z = lax.rem(place_ref[0] + dz, plan.z)
                y = lax.rem(place_ref[1] + dy, plan.y)
                c = lax.rem(place_ref[2] + dc, CORES)
                p = (z * plan.y + y) * CORES + c
                out = outs[at]
                at += 1
                for j in range(plan.blocks):
                    lanes = slice(j * LANES, (j + 1) * LANES)
                    out[:, lanes] = picked[j, pl.ds(p, block, stride=plan.positions), :].astype(jnp.bfloat16)
                tails.append(picked[plan.blocks, pl.ds(p, block, stride=plan.positions), :])
                if dy % 2:
                    out[:, main:padded] = jnp.where(left, tails[dy], tails[dy - 1]).astype(jnp.bfloat16)


def select(plan, place, index, features):
    block = 32
    slots, positions, channels = features.shape
    padded = plan.main + LANES
    kinds = [
        (dz, dc, dy) for dz in range(plan.z) for dc in range(CORES) for dy in range(plan.y)
    ]
    widths = [padded if dy % 2 else plan.main for _, _, dy in kinds]
    outs = pl.pallas_call(
        functools.partial(select_kernel, plan, block),
        grid_spec=pltpu.PrefetchScalarGridSpec(
            num_scalar_prefetch=1,
            grid=(slots // block,),
            in_specs=[
                pl.BlockSpec((1, plan.width), lambda i, s: (0, 0)),
                pl.BlockSpec((block, positions, channels), lambda i, s: (i, 0, 0)),
            ],
            out_specs=[pl.BlockSpec((block, w), lambda i, s: (i, 0)) for w in widths],
            scratch_shapes=[
                pltpu.VMEM((channels, padded), jnp.bfloat16),
                pltpu.VMEM((plan.blocks + 1, block * positions, LANES), jnp.float32),
            ],
        ),
        out_shape=[jax.ShapeDtypeStruct((slots, w), jnp.bfloat16) for w in widths],
        compiler_params=pltpu.CompilerParams(dimension_semantics=("arbitrary",)),
        cost_estimate=pl.CostEstimate(
            flops=2 * slots * positions * channels * padded,
            bytes_accessed=2 * slots * positions * (channels + padded),
            transcendentals=0,
        ),
        name="select",
    )(place, index, features)
    return dict(zip(kinds, outs))


def gram_kernel(plan, odd, count, *refs):
    mains, tails, out = refs[:count], refs[count:-1], refs[-1]
    main, tail8 = plan.main, plan.tail8
    rows = jnp.concatenate([r[:, :main] for r in mains], axis=0)
    if odd:
        last = jnp.concatenate([r[:, main:] for r in mains], axis=0)
    else:
        last = jnp.concatenate([r[...] for r in tails], axis=0)
    sub = lax.broadcasted_iota(jnp.int32, (LANES, LANES), 0)
    lane = lax.broadcasted_iota(jnp.int32, (LANES, LANES), 1)

    def put(key, value):
        at = plan.row_of[key]
        out[at : at + value.shape[0], :] = value

    held = None
    contract = (((0,), (0,)), ((), ()))
    for i in range(plan.blocks):
        left = rows[:, i * LANES : (i + 1) * LANES]
        strip = lax.dot_general(left, rows[:, i * LANES :], contract, preferred_element_type=jnp.float32)
        for j in range(i + 1, plan.blocks):
            put((i, j), strip[:, (j - i) * LANES : (j - i + 1) * LANES])
        diag = strip[:, :LANES]
        if i % 2 == 0:
            held = diag
            if i + 1 == plan.blocks:
                put((i, i), held)
        else:
            put((i - 1, i - 1), jnp.where(sub <= lane, held, diag))
            at = plan.row_of["diag"] + i // 2
            out[at : at + 1, :] = jnp.sum(jnp.where(sub == lane, diag, 0.0), axis=0, keepdims=True)
    start = 0 if odd else LANES // 2
    strip = lax.dot_general(last, rows, contract, preferred_element_type=jnp.float32)
    for j in range(plan.blocks):
        put(("tail", j), strip[start : start + tail8, j * LANES : (j + 1) * LANES])
    corner = lax.dot_general(last, last, contract, preferred_element_type=jnp.float32)
    corner = corner[start : start + tail8, :]
    if start:
        corner = jnp.concatenate([corner[:, start:], corner[:, :start]], axis=1)
    put(("tail", plan.blocks), corner)


def gram(plan, odd, mains, tails):
    whole = pl.BlockSpec(memory_space=pltpu.VMEM)
    images = sum(m.shape[0] for m in mains)
    tail_spec = pl.BlockSpec((tails[0].shape[0], LANES), lambda i: (0, plan.blocks)) if tails else None
    full = [pl.BlockSpec(m.shape, lambda i: (0, 0)) for m in mains]
    return pl.pallas_call(
        functools.partial(gram_kernel, plan, odd, len(mains)),
        grid=(1,),
        in_specs=full + [tail_spec] * len(tails),
        out_specs=pl.BlockSpec((plan.rows, LANES), lambda i: (0, 0)),
        out_shape=jax.ShapeDtypeStruct((plan.rows, LANES), jnp.float32),
        cost_estimate=pl.CostEstimate(
            flops=2 * images * plan.main * (plan.main // 2 + 2 * LANES),
            bytes_accessed=2 * images * (plan.main + LANES) + 4 * plan.rows * LANES,
            transcendentals=0,
        ),
        name="gram_odd" if odd else "gram_even",
    )(*mains, *tails)


def finish_kernel(plan, terms, place_ref, *refs):
    mine, other = refs[:terms], refs[terms : 2 * terms]
    centre_ref, covar_ref, sums = refs[2 * terms :]
    core = place_ref[2]
    sums[core] = functools.reduce(lambda a, b: a + b, [r[...] for r in mine])
    sums[CORES - 1 - core] = functools.reduce(lambda a, b: a + b, [r[...] for r in other])
    nb, tail, width, main = plan.blocks, plan.tail, plan.width, plan.main
    sub = lax.broadcasted_iota(jnp.int32, (LANES, LANES), 0)
    lane = lax.broadcasted_iota(jnp.int32, (LANES, LANES), 1)
    rest = width - main
    for p in range(CORES):
        def get(key, size):
            at = plan.row_of[key]
            return sums[p, at : at + size, :]

        def tail_row(j):
            at = plan.row_of[("tail", j)] + tail - 1
            return sums[p, at : at + 1, :]

        total = tail_row(nb)[:, tail - 1 : tail]
        centres = [tail_row(j) / total for j in range(nb + 1)]
        columns = [jnp.transpose(jnp.broadcast_to(c, (LANES, LANES))) for c in centres]
        for j in range(nb):
            centre_ref[p : p + 1, j * LANES : (j + 1) * LANES] = centres[j]
        if rest:
            centre_ref[p : p + 1, main:width] = centres[nb][:, :rest]
        lower = total - 1.0
        scale = 1.0 / lower

        def covar(sq, i, j):
            rows = sq.shape[0]
            return (sq - total * columns[i][:rows] * centres[j]) * scale

        for i in range(nb):
            for j in range(i + 1, nb):
                block = covar(get((i, j), LANES), i, j)
                covar_ref[p, i * LANES : (i + 1) * LANES, j * LANES : (j + 1) * LANES] = block
                covar_ref[p, j * LANES : (j + 1) * LANES, i * LANES : (i + 1) * LANES] = jnp.transpose(block)
        for i in range(nb):
            packed = get((i - i % 2, i - i % 2), LANES)
            flipped = jnp.transpose(packed)
            if i % 2 == 0:
                sq = jnp.where(sub <= lane, packed, flipped) if i + 1 < nb else packed
            else:
                at = plan.row_of["diag"] + i // 2
                sq = jnp.where(sub == lane, sums[p, at : at + 1, :], jnp.where(sub > lane, packed, flipped))
            block = covar(sq, i, i) + jnp.where(sub == lane, REG, 0.0)
            covar_ref[p, i * LANES : (i + 1) * LANES, i * LANES : (i + 1) * LANES] = block
        if rest:
            for j in range(nb):
                block = covar(get(("tail", j), plan.tail8), nb, j)
                covar_ref[p, main:width, j * LANES : (j + 1) * LANES] = block[:rest]
                full = jnp.concatenate([block, jnp.zeros((LANES - plan.tail8, LANES), jnp.float32)], axis=0)
                covar_ref[p, j * LANES : (j + 1) * LANES, main:width] = jnp.transpose(full)[:, :rest]
            t8 = plan.tail8
            block = covar(get(("tail", nb), t8), nb, nb) + jnp.where(sub[:t8] == lane[:t8], REG, 0.0)
            covar_ref[p, main:width, main:width] = block[:rest, :rest]


def finish(plan, place, mine, other):
    width = plan.width
    spec = pl.BlockSpec((plan.rows, LANES), lambda i, s: (0, 0))
    return pl.pallas_call(
        functools.partial(finish_kernel, plan, len(mine)),
        grid_spec=pltpu.PrefetchScalarGridSpec(
            num_scalar_prefetch=1,
            grid=(1,),
            in_specs=[spec] * (2 * len(mine)),
            out_specs=[
                pl.BlockSpec((CORES, width), lambda i, s: (0, 0)),
                pl.BlockSpec((CORES, width, width), lambda i, s: (0, 0, 0)),
            ],
            scratch_shapes=[pltpu.VMEM((CORES, plan.rows, LANES), jnp.float32)],
        ),
        out_shape=[
            jax.ShapeDtypeStruct((CORES, width), jnp.float32),
            jax.ShapeDtypeStruct((CORES, width, width), jnp.float32),
        ],
        name="finish",
    )(place, *mine, *other)


def body(mesh, features, channel_index, image_counts):
    plan = Plan(mesh, features.shape[0], features.shape[1], channel_index.shape[0])
    img, pos = lax.axis_index("img"), lax.axis_index("pos")
    place = jnp.stack([pos // plan.y, pos % plan.y, img % CORES, image_counts[0]]).astype(jnp.int32)
    sent = select(plan, place, channel_index[None, :], features)
    order = [(dz, dc) for dz in range(plan.z) for dc in range(CORES)]
    got = {
        (dz, dc, dy): plan.send(sent[dz, dc, dy], dz=dz, dc=dc)
        for dy in range(plan.y - 1, -1, -1)
        for dz, dc in order
    }
    partial = {}
    for dy in range(plan.y - 1, -1, -1):
        mains = [got[dz, dc, dy] for dz, dc in order]
        tails = [] if dy % 2 else [got[dz, dc, dy + 1] for dz, dc in order]
        partial[dy] = gram(plan, bool(dy % 2), mains, tails)
    mine = partial[0]
    for dy in range(1, plan.y):
        mine = mine + plan.send(partial[dy], dy=dy)
    terms = [mine] + [plan.send(mine, dx=dx) for dx in range(1, plan.x)]
    total = functools.reduce(lambda a, b: a + b, terms)
    swapped = plan.send(total, dc=1)
    return finish(plan, place, [total], [swapped])


def solution(mesh):
    placed = (P(("img", "pos"), None, None), P(), P(("img", "pos")))
    return jax.shard_map(
        functools.partial(body, mesh),
        mesh=mesh,
        in_specs=placed,
        out_specs=(P("pos", None), P("pos", None, None)),
        check_vma=False,
    )
```

```python
import functools
import itertools

import jax
import jax.numpy as jnp
from jax import lax
from jax.experimental import pallas as pl
from jax.experimental.pallas import tpu as pltpu
from jax.sharding import PartitionSpec as P


REG = 0.01
LANES = 128
CORES = 2
AXES = ("img", "pos")


def ceil_to(n, m):
    return -(-n // m) * m


class Plan:
    def __init__(self, mesh, slots, positions, width):
        images, owners = mesh.shape["img"], mesh.shape["pos"]
        self.near = 2
        self.far = images // CORES // self.near
        self.y = 1
        while (self.y * 2) ** 2 <= owners and owners % (self.y * 2) == 0:
            self.y *= 2
        self.halves = 2
        self.low = owners // self.y // self.halves
        assert images == self.far * self.near * CORES
        assert owners == self.halves * self.low * self.y and positions == owners * self.near
        self.slots, self.width = slots, width
        self.group = positions // self.halves
        self.blocks = (width + 1) // LANES
        self.main = self.blocks * LANES
        self.padded = self.main + LANES
        self.tail = width + 1 - self.main
        self.tail8 = ceil_to(self.tail, 8)
        self.row_of = {}
        at = 0
        for i in range(self.blocks):
            for j in range(i + 1, self.blocks):
                self.row_of[(i, j)] = at
                at += LANES
        for i in range(0, self.blocks, 2):
            self.row_of[(i, i)] = at
            at += LANES
        for j in range(self.blocks + 1):
            self.row_of[("tail", j)] = at
            at += self.tail8
        self.row_of["diag"] = at
        self.rows = ceil_to(at + -(-self.blocks // 2), 8 * CORES)
        self.part = self.rows // CORES
        self.steps = [
            (dx, dl, dy) for dx in range(self.near) for dl in range(self.low) for dy in range(self.y)
        ]

    def moved(self, far=0, near=0, core=0, half=0, low=0, y=0):
        sizes = (self.far, self.near, CORES, self.halves, self.low, self.y)
        shift = (far, near, core, half, low, y)
        pairs = []
        for here in itertools.product(*map(range, sizes)):
            to = [(h + d) % n for h, d, n in zip(here, shift, sizes)]
            index = lambda at: functools.reduce(lambda a, b: a * b[1] + b[0], zip(at, sizes), 0)
            pairs.append((index(here), index(to)))
        return pairs

    def send(self, value, **step):
        if not any(step.values()):
            return value
        return lax.ppermute(value, AXES, self.moved(**step))


def select_kernel(plan, block, place_ref, index_ref, x_ref, *refs):
    outs, (onehot, picked) = refs[:-2], refs[-2:]
    step = pl.program_id(0)
    channels = x_ref.shape[2]
    main, tail = plan.main, plan.tail

    @pl.when(step == 0)
    def _():
        rows = lax.broadcasted_iota(jnp.int32, (channels, LANES), 0)
        for j in range(plan.blocks):
            at = slice(j * LANES, (j + 1) * LANES)
            onehot[:, at] = jnp.where(rows == index_ref[:, at], 1.0, 0.0).astype(jnp.bfloat16)
        last = index_ref[:, main : plan.width]
        last = jnp.concatenate([last, jnp.full((1, LANES - last.shape[1]), -1, jnp.int32)], axis=1)
        onehot[:, main:] = jnp.where(rows == last, 1.0, 0.0).astype(jnp.bfloat16)

    x = x_ref[...].reshape(block * plan.group, channels)
    got = jnp.dot(x, onehot[...], preferred_element_type=jnp.float32)
    image = step * block + lax.broadcasted_iota(jnp.int32, (block * plan.group, 1), 0) // plan.group
    used = image < place_ref[4]
    ones = lax.broadcasted_iota(jnp.int32, (1, plan.padded), 1) == main + tail - 1
    got = jnp.where(used, jnp.where(ones, 1.0, got), 0.0)
    for j in range(plan.blocks + 1):
        picked[j] = got[:, j * LANES : (j + 1) * LANES]
    for out, (dx, dl, dy) in zip(outs, plan.steps):
        near = lax.rem(place_ref[0] + dx, plan.near)
        low = lax.rem(place_ref[1] + dl, plan.low)
        y = lax.rem(place_ref[2] + dy, plan.y)
        p = (low * plan.y + y) * plan.near + near
        for j in range(plan.blocks + 1):
            lanes = slice(j * LANES, (j + 1) * LANES)
            out[:, lanes] = picked[j, pl.ds(p, block, stride=plan.group), :].astype(jnp.bfloat16)


def select(plan, place, flip, index, features):
    block = 32
    slots, _, channels = features.shape
    count = len(plan.steps)
    outs = pl.pallas_call(
        functools.partial(select_kernel, plan, block),
        grid_spec=pltpu.PrefetchScalarGridSpec(
            num_scalar_prefetch=1,
            grid=(slots // block,),
            in_specs=[
                pl.BlockSpec((1, plan.width), lambda i, s: (0, 0)),
                pl.BlockSpec(
                    (block, plan.group, channels),
                    lambda i, s: (i, lax.rem(s[3] + flip, plan.halves), 0),
                ),
            ],
            out_specs=[pl.BlockSpec((block, plan.padded), lambda i, s: (i, 0))] * count,
            scratch_shapes=[
                pltpu.VMEM((channels, plan.padded), jnp.bfloat16),
                pltpu.VMEM((plan.blocks + 1, block * plan.group, LANES), jnp.float32),
            ],
        ),
        out_shape=[jax.ShapeDtypeStruct((slots, plan.padded), jnp.bfloat16)] * count,
        compiler_params=pltpu.CompilerParams(
            dimension_semantics=("arbitrary",), vmem_limit_bytes=56 << 20
        ),
        cost_estimate=pl.CostEstimate(
            flops=2 * slots * plan.group * channels * plan.padded,
            bytes_accessed=2 * slots * plan.group * (channels + plan.padded),
            transcendentals=0,
        ),
        name="select_other" if flip else "select_own",
    )(place, index, features)
    return dict(zip(plan.steps, outs))


def gram_kernel(plan, place_ref, *refs):
    ins, (keep, give, out) = refs[:-3], refs[-3:]
    main, tail8 = plan.main, plan.tail8
    rows = jnp.concatenate([r[:, :main] for r in ins], axis=0)
    last = jnp.concatenate([r[:, main:] for r in ins], axis=0)
    sub = lax.broadcasted_iota(jnp.int32, (LANES, LANES), 0)
    lane = lax.broadcasted_iota(jnp.int32, (LANES, LANES), 1)

    def put(key, value):
        at = plan.row_of[key]
        out[at : at + value.shape[0], :] = value

    held = None
    contract = (((0,), (0,)), ((), ()))
    for i in range(plan.blocks):
        left = rows[:, i * LANES : (i + 1) * LANES]
        strip = lax.dot_general(left, rows[:, i * LANES :], contract, preferred_element_type=jnp.float32)
        for j in range(i + 1, plan.blocks):
            put((i, j), strip[:, (j - i) * LANES : (j - i + 1) * LANES])
        diag = strip[:, :LANES]
        if i % 2 == 0:
            held = diag
            if i + 1 == plan.blocks:
                put((i, i), held)
        else:
            put((i - 1, i - 1), jnp.where(sub <= lane, held, diag))
            at = plan.row_of["diag"] + i // 2
            out[at : at + 1, :] = jnp.sum(jnp.where(sub == lane, diag, 0.0), axis=0, keepdims=True)
    strip = lax.dot_general(last, rows, contract, preferred_element_type=jnp.float32)
    for j in range(plan.blocks):
        put(("tail", j), strip[:tail8, j * LANES : (j + 1) * LANES])
    corner = lax.dot_general(last, last, contract, preferred_element_type=jnp.float32)
    put(("tail", plan.blocks), corner[:tail8])
    unused = plan.row_of["diag"] + plan.blocks // 2
    out[unused:, :] = jnp.zeros((plan.rows - unused, LANES), jnp.float32)
    core = place_ref[5]
    first = pl.multiple_of(core * plan.part, 8)
    second = pl.multiple_of((CORES - 1 - core) * plan.part, 8)
    keep[...] = out[pl.ds(first, plan.part), :]
    give[...] = out[pl.ds(second, plan.part), :]


def gram(plan, place, rows):
    images = sum(m.shape[0] for m in rows)
    part = jax.ShapeDtypeStruct((plan.part, LANES), jnp.float32)
    return pl.pallas_call(
        functools.partial(gram_kernel, plan),
        grid_spec=pltpu.PrefetchScalarGridSpec(
            num_scalar_prefetch=1,
            grid=(1,),
            in_specs=[pl.BlockSpec(m.shape, lambda i, s: (0, 0)) for m in rows],
            out_specs=[pl.BlockSpec(part.shape, lambda i, s: (0, 0))] * 2,
            scratch_shapes=[pltpu.VMEM((plan.rows, LANES), jnp.float32)],
        ),
        out_shape=[part, part],
        compiler_params=pltpu.CompilerParams(vmem_limit_bytes=24 << 20),
        cost_estimate=pl.CostEstimate(
            flops=2 * images * plan.main * (plan.main // 2 + 2 * LANES),
            bytes_accessed=2 * images * plan.padded + 4 * plan.rows * LANES,
            transcendentals=0,
        ),
    )(place, *rows)


def finish_kernel(plan, place_ref, *refs):
    parts, (centre_ref, covar_ref, sums) = refs[:4], refs[4:]
    near, core = place_ref[0], place_ref[5]
    for at, part in enumerate(parts):
        p = near if at % 2 == 0 else plan.near - 1 - near
        c = core if at // 2 == 0 else CORES - 1 - core
        sums[p, pl.ds(pl.multiple_of(c * plan.part, 8), plan.part), :] = part[...]
    nb, tail, width, main = plan.blocks, plan.tail, plan.width, plan.main
    sub = lax.broadcasted_iota(jnp.int32, (LANES, LANES), 0)
    lane = lax.broadcasted_iota(jnp.int32, (LANES, LANES), 1)
    rest = width - main
    for p in range(plan.near):
        def get(key, size):
            at = plan.row_of[key]
            return sums[p, at : at + size, :]

        def tail_row(j):
            at = plan.row_of[("tail", j)] + tail - 1
            return sums[p, at : at + 1, :]

        total = tail_row(nb)[:, tail - 1 : tail]
        centres = [tail_row(j) / total for j in range(nb + 1)]
        columns = [jnp.transpose(jnp.broadcast_to(c, (LANES, LANES))) for c in centres]
        for j in range(nb):
            centre_ref[p : p + 1, j * LANES : (j + 1) * LANES] = centres[j]
        if rest:
            centre_ref[p : p + 1, main:width] = centres[nb][:, :rest]
        lower = total - 1.0
        scale = 1.0 / lower

        def covar(sq, i, j):
            rows = sq.shape[0]
            return (sq - total * columns[i][:rows] * centres[j]) * scale

        for i in range(nb):
            for j in range(i + 1, nb):
                block = covar(get((i, j), LANES), i, j)
                covar_ref[p, i * LANES : (i + 1) * LANES, j * LANES : (j + 1) * LANES] = block
                covar_ref[p, j * LANES : (j + 1) * LANES, i * LANES : (i + 1) * LANES] = jnp.transpose(block)
        for i in range(nb):
            packed = get((i - i % 2, i - i % 2), LANES)
            flipped = jnp.transpose(packed)
            if i % 2 == 0:
                sq = jnp.where(sub <= lane, packed, flipped) if i + 1 < nb else packed
            else:
                at = plan.row_of["diag"] + i // 2
                sq = jnp.where(sub == lane, sums[p, at : at + 1, :], jnp.where(sub > lane, packed, flipped))
            block = covar(sq, i, i) + jnp.where(sub == lane, REG, 0.0)
            covar_ref[p, i * LANES : (i + 1) * LANES, i * LANES : (i + 1) * LANES] = block
        if rest:
            for j in range(nb):
                block = covar(get(("tail", j), plan.tail8), nb, j)
                covar_ref[p, main:width, j * LANES : (j + 1) * LANES] = block[:rest]
                full = jnp.concatenate([block, jnp.zeros((LANES - plan.tail8, LANES), jnp.float32)], axis=0)
                covar_ref[p, j * LANES : (j + 1) * LANES, main:width] = jnp.transpose(full)[:, :rest]
            t8 = plan.tail8
            block = covar(get(("tail", nb), t8), nb, nb) + jnp.where(sub[:t8] == lane[:t8], REG, 0.0)
            covar_ref[p, main:width, main:width] = block[:rest, :rest]


def finish(plan, place, parts):
    width = plan.width
    return pl.pallas_call(
        functools.partial(finish_kernel, plan),
        grid_spec=pltpu.PrefetchScalarGridSpec(
            num_scalar_prefetch=1,
            grid=(1,),
            in_specs=[pl.BlockSpec((plan.part, LANES), lambda i, s: (0, 0))] * 4,
            out_specs=[
                pl.BlockSpec((plan.near, width), lambda i, s: (0, 0)),
                pl.BlockSpec((plan.near, width, width), lambda i, s: (0, 0, 0)),
            ],
            scratch_shapes=[pltpu.VMEM((plan.near, plan.rows, LANES), jnp.float32)],
        ),
        out_shape=[
            jax.ShapeDtypeStruct((plan.near, width), jnp.float32),
            jax.ShapeDtypeStruct((plan.near, width, width), jnp.float32),
        ],
        compiler_params=pltpu.CompilerParams(vmem_limit_bytes=24 << 20),
        name="finish",
    )(place, *parts)


def body(mesh, features, channel_index, image_counts):
    plan = Plan(mesh, features.shape[0], features.shape[1], channel_index.shape[0])
    img, pos = lax.axis_index("img"), lax.axis_index("pos")
    place = jnp.stack(
        [
            img // CORES % plan.near,
            pos // plan.y % plan.low,
            pos % plan.y,
            pos // (plan.y * plan.low),
            image_counts[0],
            img % CORES,
        ]
    ).astype(jnp.int32)
    index = channel_index[None, :]

    def exchange(sent):
        return [plan.send(sent[step], near=step[0], low=step[1], y=step[2]) for step in plan.steps]

    sent_other = select(plan, place, 1, index, features)
    sent_own = select(plan, place, 0, index, features)
    got_other = exchange(sent_other)
    got_own = exchange(sent_own)
    keep, give = gram(plan, place, got_other)
    took = plan.send(give, core=1)
    other = keep + took
    crossed = plan.send(other, half=1)
    keep, give = gram(plan, place, got_own)
    took = plan.send(give, core=1)
    total = own = keep + took + crossed
    for step in range(1, plan.far):
        total = total + plan.send(own, far=step)
    across = plan.send(total, near=1)
    swapped = plan.send(total, core=1)
    swapped_across = plan.send(across, core=1)
    return finish(plan, place, [total, across, swapped, swapped_across])


def solution(mesh):
    placed = (P(("img", "pos"), None, None), P(), P(("img", "pos")))

    def layer(*args):
        return body(mesh, *args)

    return jax.shard_map(
        layer,
        mesh=mesh,
        in_specs=placed,
        out_specs=(P("pos", None), P("pos", None, None)),
        check_vma=False,
    )
```

```python
import collections
import functools
import itertools

import jax
import jax.numpy as jnp
from jax import lax
from jax.experimental import pallas as pl
from jax.experimental.pallas import tpu as pltpu
from jax.sharding import PartitionSpec as P


REG = 0.01
LANES = 128
CORES = 2
PACK = 16
PIECES = 2
STEPS = 4
LIMIT = 44
AXES = ("img", "pos")


def ceil_to(n, m):
    return -(-n // m) * m


Here = collections.namedtuple("Here", ["near", "core", "half", "low", "y"])


def OWN_ORDER(step):
    dx, dl, dy = map(bool, step)
    return [0b000, 0b001, 0b100, 0b010, 0b101, 0b011, 0b110, 0b111].index(dx << 2 | dl << 1 | dy)


class Plan:
    def __init__(self, mesh):
        images, self.owners = mesh.shape["img"], mesh.shape["pos"]
        self.near = 2
        self.far = images // CORES // self.near
        self.y = 1
        while (self.y * 2) ** 2 <= self.owners and self.owners % (self.y * 2) == 0:
            self.y *= 2
        self.halves = 2
        self.low = self.owners // self.y // self.halves
        assert images == self.far * self.near * CORES
        assert self.owners == self.halves * self.low * self.y
        steps = list(itertools.product(range(self.near), range(self.low), range(self.y)))
        hops = lambda s: sum(map(bool, s))
        self.steps = sorted(steps, key=lambda s: (hops(s), s[1] > 0, s[0] > 0))
        self.own_steps = sorted(steps, key=OWN_ORDER)

    def fit(self, slots, positions, width):
        assert positions == self.owners * self.near and slots == LANES
        self.slots, self.width = slots, width
        self.group = positions // self.halves
        self.blocks = (width + 1) // LANES
        self.main = self.blocks * LANES
        self.padded = self.main + LANES
        self.tail = width + 1 - self.main
        self.tail8 = ceil_to(self.tail, 8)
        self.tail_tiles = ceil_to(self.tail, PACK) // PACK
        self.message = (slots + PACK, self.main)
        assert self.tail_tiles <= self.blocks
        self.row_of = {}
        at = 0
        for i in range(self.blocks):
            for j in range(i + 1, self.blocks):
                self.row_of[(i, j)] = at
                at += LANES
        for i in range(0, self.blocks, 2):
            self.row_of[(i, i)] = at
            at += LANES
        for j in range(self.blocks + 1):
            self.row_of[("tail", j)] = at
            at += self.tail8
        self.row_of["diag"] = at
        self.rows = ceil_to(at + -(-self.blocks // 2), 8 * CORES)
        self.part = self.rows // CORES
        sizes = [self.part // 8 // PIECES + (k < self.part // 8 % PIECES) for k in range(PIECES)]
        ends = [8 * e for e in itertools.accumulate(sizes)]
        self.cuts = [slice(e - 8 * n, e) for e, n in zip(ends, sizes)]

    def moved(self, far=0, near=0, core=0, half=0, low=0, y=0):
        sizes = (self.far, self.near, CORES, self.halves, self.low, self.y)
        shift = (far, near, core, half, low, y)
        pairs = []
        for here in itertools.product(*map(range, sizes)):
            to = [(h + d) % n for h, d, n in zip(here, shift, sizes)]
            index = lambda at: functools.reduce(lambda a, b: a * b[1] + b[0], zip(at, sizes), 0)
            pairs.append((index(here), index(to)))
        return pairs

    def here(self):
        img, pos = lax.axis_index("img"), lax.axis_index("pos")
        return Here(
            near=lax.rem(img // CORES, self.near),
            core=lax.rem(img, CORES),
            half=pos // (self.y * self.low),
            low=lax.rem(pos // self.y, self.low),
            y=lax.rem(pos, self.y),
        )

    def send(self, value, **step):
        if not any(step.values()):
            return value
        return lax.ppermute(value, AXES, self.moved(**step))


def pick(plan, xs, hot, counts_ref, outs, picked, tails, wait):
    slots, _, channels = xs.shape
    block = slots // STEPS
    at = plan.here()
    ones = lax.broadcasted_iota(jnp.int32, (1, plan.padded), 1) == plan.width
    image = lax.broadcasted_iota(jnp.int32, (block * plan.group, 1), 0) // plan.group
    for step in range(STEPS):
        wait(step)
        images = slice(step * block, (step + 1) * block)
        x = xs[images].reshape(block * plan.group, channels)
        got = jnp.dot(x, hot[...], preferred_element_type=jnp.float32)
        got = jnp.where(image < counts_ref[0] - step * block, jnp.where(ones, 1.0, got), 0.0)
        slot = step % 2
        for j in range(plan.blocks + 1):
            picked[slot, j] = got[:, j * LANES : (j + 1) * LANES]
        for k, (out, (dx, dl, dy)) in enumerate(zip(outs, plan.steps)):
            near = lax.rem(at.near + dx, plan.near)
            low = lax.rem(at.low + dl, plan.low)
            y = lax.rem(at.y + dy, plan.y)
            p = (low * plan.y + y) * plan.near + near
            rows = pl.ds(p, block, stride=plan.group)
            for j in range(plan.blocks):
                out[images, j * LANES : (j + 1) * LANES] = picked[slot, j, rows, :].astype(jnp.bfloat16)
            tails[k, images, :] = picked[slot, plan.blocks, rows, :]
    for k, out in enumerate(outs):
        flipped = jnp.transpose(tails[k]).astype(jnp.bfloat16)
        for t in range(plan.tail_tiles):
            out[slots:, t * LANES : (t + 1) * LANES] = flipped[t * PACK : (t + 1) * PACK]
        if plan.tail_tiles < plan.blocks:
            out[slots:, plan.tail_tiles * LANES :] = jnp.zeros(
                (PACK, plan.main - plan.tail_tiles * LANES), jnp.bfloat16
            )


def select_other_kernel(plan, counts_ref, index_hbm, x_hbm, *refs):
    outs, (own, hot), (other, index_ref, picked, tails, sems) = refs[:-7], refs[-7:-5], refs[-5:]
    slots, _, channels = own.shape
    block = slots // STEPS
    half = plan.here().half

    def fetch(flip, step):
        images = pl.ds(step * block, block)
        first = lax.rem(half + flip, plan.halves) * plan.group
        group = pl.ds(pl.multiple_of(first, plan.group), plan.group)
        to = other if flip else own
        return pltpu.make_async_copy(x_hbm.at[images, group, :], to.at[images], sems.at[flip, step])

    fetch_index = pltpu.make_async_copy(index_hbm, index_ref, sems.at[0, STEPS])
    fetch_index.start()
    for flip in (1, 0):
        for step in range(STEPS):
            fetch(flip, step).start()
    fetch_index.wait()
    index = index_ref[...].reshape(1, plan.width)
    rows = lax.broadcasted_iota(jnp.int32, (channels, LANES), 0)
    for j in range(plan.blocks + 1):
        lanes = index[:, j * LANES : min((j + 1) * LANES, plan.width)]
        if lanes.shape[1] < LANES:
            lanes = jnp.concatenate([lanes, jnp.full((1, LANES - lanes.shape[1]), -1, jnp.int32)], axis=1)
        hot[:, j * LANES : (j + 1) * LANES] = jnp.where(rows == lanes, 1.0, 0.0).astype(jnp.bfloat16)
    pick(plan, other, hot, counts_ref, outs, picked, tails, lambda step: fetch(1, step).wait())
    for step in range(STEPS):
        fetch(0, step).wait()


def select_own_kernel(plan, counts_ref, own, hot, *refs):
    outs, (picked, tails) = refs[:-2], refs[-2:]
    pick(plan, own, hot, counts_ref, outs, picked, tails, lambda step: None)


def select(plan, kernel, inputs, kept, scratch, channels):
    count = len(plan.steps)
    vmem, anywhere = pl.BlockSpec(memory_space=pltpu.VMEM), pl.BlockSpec(memory_space=pl.ANY)
    first = bool(kept)
    outs = pl.pallas_call(
        functools.partial(kernel, plan),
        in_specs=[pl.BlockSpec(memory_space=pltpu.SMEM)] + [anywhere if first else vmem] * 2,
        out_specs=[vmem] * (count + len(kept)),
        scratch_shapes=scratch
        + [
            pltpu.VMEM((2, plan.blocks + 1, plan.slots // STEPS * plan.group, LANES), jnp.float32),
            pltpu.VMEM((count, plan.slots, LANES), jnp.float32),
        ]
        + ([pltpu.SemaphoreType.DMA((2, STEPS + 1))] if first else []),
        out_shape=[jax.ShapeDtypeStruct(plan.message, jnp.bfloat16)] * count + kept,
        compiler_params=pltpu.CompilerParams(vmem_limit_bytes=LIMIT << 20),
        cost_estimate=pl.CostEstimate(
            flops=2 * plan.slots * plan.group * channels * plan.padded,
            bytes_accessed=2 * plan.slots * plan.group * (channels + plan.padded),
            transcendentals=0,
        ),
    )(*inputs)
    return dict(zip(plan.steps, outs)), outs[count:]


def select_other(plan, counts, index, features):
    slots, _, channels = features.shape
    half = (slots, plan.group, channels)
    return select(
        plan,
        select_other_kernel,
        (counts, *(pltpu.with_memory_space_constraint(v, pltpu.HBM) for v in (index, features))),
        [
            jax.ShapeDtypeStruct(half, features.dtype),
            jax.ShapeDtypeStruct((channels, plan.padded), jnp.bfloat16),
        ],
        [pltpu.VMEM(half, features.dtype), pltpu.VMEM((plan.width,), jnp.int32)],
        channels,
    )


def select_own(plan, counts, own, hot):
    return select(plan, select_own_kernel, (counts, own, hot), [], [], own.shape[2])[0]


def gram_kernel(plan, *refs):
    ins, (keep, give, out) = refs[:-3], refs[-3:]
    tail8 = plan.tail8
    slots = ins[0].shape[0] - PACK
    rows = jnp.concatenate([r[:slots, :] for r in ins], axis=0)
    tiles = [slice(t * LANES, (t + 1) * LANES) for t in range(plan.tail_tiles)]
    last = jnp.concatenate(
        [jnp.concatenate([r[slots:, t] for t in tiles], axis=0) for r in ins], axis=1
    )
    sub = lax.broadcasted_iota(jnp.int32, (LANES, LANES), 0)
    lane = lax.broadcasted_iota(jnp.int32, (LANES, LANES), 1)

    def put(key, value):
        at = plan.row_of[key]
        out[at : at + value.shape[0], :] = value

    held = None
    contract = (((0,), (0,)), ((), ()))
    for i in range(plan.blocks):
        left = rows[:, i * LANES : (i + 1) * LANES]
        strip = lax.dot_general(left, rows[:, i * LANES :], contract, preferred_element_type=jnp.float32)
        for j in range(i + 1, plan.blocks):
            put((i, j), strip[:, (j - i) * LANES : (j - i + 1) * LANES])
        diag = strip[:, :LANES]
        if i % 2 == 0:
            held = diag
            if i + 1 == plan.blocks:
                put((i, i), held)
        else:
            put((i - 1, i - 1), jnp.where(sub <= lane, held, diag))
            at = plan.row_of["diag"] + i // 2
            out[at : at + 1, :] = jnp.sum(jnp.where(sub == lane, diag, 0.0), axis=0, keepdims=True)
    strip = jnp.dot(last, rows, preferred_element_type=jnp.float32)
    for j in range(plan.blocks):
        put(("tail", j), strip[:tail8, j * LANES : (j + 1) * LANES])
    full = jnp.concatenate([last, jnp.zeros((LANES - last.shape[0], last.shape[1]), last.dtype)], axis=0)
    corner = lax.dot_general(
        last, full, (((1,), (1,)), ((), ())), preferred_element_type=jnp.float32
    )
    put(("tail", plan.blocks), corner[:tail8])
    unused = plan.row_of["diag"] + plan.blocks // 2
    out[unused:, :] = jnp.zeros((plan.rows - unused, LANES), jnp.float32)
    core = plan.here().core
    first = pl.multiple_of(core * plan.part, 8)
    second = pl.multiple_of((CORES - 1 - core) * plan.part, 8)
    keep[...] = out[pl.ds(first, plan.part), :]
    give[...] = out[pl.ds(second, plan.part), :]


def gram(plan, rows):
    images = plan.slots * len(rows)
    part = jax.ShapeDtypeStruct((plan.part, LANES), jnp.float32)
    return pl.pallas_call(
        functools.partial(gram_kernel, plan),
        in_specs=[pl.BlockSpec(memory_space=pltpu.VMEM)] * len(rows),
        out_specs=[pl.BlockSpec(memory_space=pltpu.VMEM)] * 2,
        scratch_shapes=[pltpu.VMEM((plan.rows, LANES), jnp.float32)],
        out_shape=[part, part],
        compiler_params=pltpu.CompilerParams(vmem_limit_bytes=24 << 20),
        cost_estimate=pl.CostEstimate(
            flops=2 * images * plan.main * (plan.main // 2 + 2 * LANES),
            bytes_accessed=2 * images * plan.padded + 4 * plan.rows * LANES,
            transcendentals=0,
        ),
    )(*rows)


def finish_kernel(plan, mine, count, *refs):
    parts, (centre_ref, covar_ref) = refs[:count], refs[-6:-4]
    sums, dense, centre_row, sems = refs[-4:]
    here = plan.here()
    for at, part in enumerate(parts):
        cut = plan.cuts[at % PIECES]
        c = here.core if at < PIECES else CORES - 1 - here.core
        sums[pl.ds(pl.multiple_of(c * plan.part + cut.start, 8), cut.stop - cut.start), :] = part[...]
    nb, tail, width, main = plan.blocks, plan.tail, plan.width, plan.main
    position = here.near if mine else plan.near - 1 - here.near
    sub = lax.broadcasted_iota(jnp.int32, (LANES, LANES), 0)
    lane = lax.broadcasted_iota(jnp.int32, (LANES, LANES), 1)
    rest = width - main

    def get(key, size):
        at = plan.row_of[key]
        return sums[at : at + size, :]

    def tail_row(j):
        at = plan.row_of[("tail", j)] + tail - 1
        return sums[at : at + 1, :]

    def copies(p, strip):
        if strip is None:
            return pltpu.make_async_copy(centre_row.at[0], centre_ref.at[p], sems.at[nb + 1])
        rows = pl.ds(strip * LANES, min(LANES, width - strip * LANES))
        return pltpu.make_async_copy(dense.at[rows], covar_ref.at[rows, p, :], sems.at[strip])

    def send(strip):
        for p in range(plan.near):

            @pl.when(position == p)
            def _():
                copies(p, strip).start()

    total = tail_row(nb)[:, tail - 1 : tail]
    centres = [tail_row(j) / total for j in range(nb + 1)]
    columns = [jnp.transpose(jnp.broadcast_to(c, (LANES, LANES))) for c in centres]
    for j in range(nb):
        centre_row[:, j * LANES : (j + 1) * LANES] = centres[j]
    if rest:
        centre_row[:, main:width] = centres[nb][:, :rest]
    send(None)
    scale = 1.0 / (total - 1.0)

    def covar(sq, i, j):
        rows = sq.shape[0]
        return (sq - total * columns[i][:rows] * centres[j]) * scale

    for i in range(nb):
        at_i = slice(i * LANES, (i + 1) * LANES)
        pair = i - i % 2
        packed = get((pair, pair), LANES)
        flipped = jnp.transpose(packed)
        if i % 2 == 0:
            sq = jnp.where(sub <= lane, packed, flipped) if i + 1 < nb else packed
        else:
            at = plan.row_of["diag"] + i // 2
            sq = jnp.where(sub == lane, sums[at : at + 1, :], jnp.where(sub > lane, packed, flipped))
        dense[at_i, at_i] = covar(sq, i, i) + jnp.where(sub == lane, REG, 0.0)
        for j in range(i + 1, nb):
            at_j = slice(j * LANES, (j + 1) * LANES)
            block = covar(get((i, j), LANES), i, j)
            dense[at_i, at_j] = block
            dense[at_j, at_i] = jnp.transpose(block)
        if rest:
            block = covar(get(("tail", i), plan.tail8), nb, i)
            dense[main:width, at_i] = block[:rest]
            full = jnp.concatenate([block, jnp.zeros((LANES - plan.tail8, LANES), jnp.float32)], axis=0)
            dense[at_i, main:width] = jnp.transpose(full)[:, :rest]
        send(i)
    if rest:
        t8 = plan.tail8
        block = covar(get(("tail", nb), t8), nb, nb) + jnp.where(sub[:t8] == lane[:t8], REG, 0.0)
        dense[main:width, main:width] = block[:rest, :rest]
        send(nb)
    for strip in [None, *range(nb + bool(rest))]:
        copies(0, strip).wait()


def finish(plan, mine, parts, before=()):
    width, nb = plan.width, plan.blocks
    anywhere = pl.BlockSpec(memory_space=pl.ANY)
    count = len(parts)
    return pl.pallas_call(
        functools.partial(finish_kernel, plan, mine, count),
        in_specs=[pl.BlockSpec(memory_space=pltpu.VMEM)] * count + [anywhere] * len(before),
        out_specs=[anywhere] * 2,
        scratch_shapes=[
            pltpu.VMEM((plan.rows, LANES), jnp.float32),
            pltpu.VMEM((width, width), jnp.float32),
            pltpu.VMEM((1, width), jnp.float32),
            pltpu.SemaphoreType.DMA((nb + 2,)),
        ],
        out_shape=[
            jax.ShapeDtypeStruct((plan.near, width), jnp.float32),
            jax.ShapeDtypeStruct((width, plan.near, width), jnp.float32),
        ],
        input_output_aliases={count + i: i for i in range(len(before))},
        compiler_params=pltpu.CompilerParams(vmem_limit_bytes=24 << 20),
        cost_estimate=pl.CostEstimate(
            flops=8 * width * width, bytes_accessed=8 * width * width, transcendentals=0
        ),
        name="finish_mine" if mine else "finish_other",
    )(*parts, *before)


def body(plan, features, channel_index, image_counts):
    plan.fit(features.shape[0], features.shape[1], channel_index.shape[0])

    def exchange(sent, steps):
        got = []
        for step in steps:
            got.append(plan.send(sent[step], near=step[0], low=step[1], y=step[2]))
        return got

    sent_other, (own, hot) = select_other(plan, image_counts, channel_index, features)
    sent_own = select_own(plan, image_counts, own, hot)
    got_other = exchange(sent_other, plan.steps)
    got_own = exchange(sent_own, plan.own_steps)
    keep, give = gram(plan, got_other)
    took = plan.send(give, core=1)
    crossed = []
    for cut in plan.cuts:
        other = keep[cut] + took[cut]
        crossed.append(plan.send(other, half=1))
    keep, give = gram(plan, got_own)
    took = plan.send(give, core=1)
    mine, other = [], []
    for k, cut in enumerate(plan.cuts):
        total = own = keep[cut] + took[cut] + crossed[k]
        for step in range(1, plan.far):
            total = total + plan.send(own, far=step)
        mine.append(total)
        other.append(plan.send(total, near=1))
    for k in range(PIECES):
        mine.append(plan.send(mine[k], core=1))
    for k in range(PIECES):
        other.append(plan.send(other[k], core=1))
    before = finish(plan, True, mine)
    centre, covar = finish(plan, False, other, before)
    return centre, jnp.transpose(covar, (1, 0, 2))


def solution(mesh):
    placed = (P(("img", "pos"), None, None), P(), P(("img", "pos")))
    plan = Plan(mesh)

    def layer(*args):
        return body(plan, *args)

    return jax.shard_map(
        layer,
        mesh=mesh,
        in_specs=placed,
        out_specs=(P("pos", None), P("pos", None, None)),
        check_vma=False,
    )
```

```python
import collections
import functools
import itertools

import jax
import jax.numpy as jnp
from jax import lax
from jax.experimental import pallas as pl
from jax.experimental.pallas import tpu as pltpu
from jax.sharding import PartitionSpec as P


REG = 0.01
LANES = 128
CORES = 2
PACK = 16
PIECES = 2
STEPS = 4
LIMIT = 44
AXES = ("img", "pos")


def ceil_to(n, m):
    return -(-n // m) * m


Here = collections.namedtuple("Here", ["near", "core", "half", "low", "y"])


OTHER_ORDER = ["", "z", "y", "x", "yz", "xz", "xyz", "xy"]
OWN_ORDER = ["", "z", "yz", "xz", "xyz", "x", "xy", "y"]


def rank(order):
    def key(step):
        dx, dl, dy = step
        return order.index("x" * bool(dx) + "y" * bool(dy) + "z" * bool(dl)), step

    return key


class Plan:
    def __init__(self, mesh):
        images, self.owners = mesh.shape["img"], mesh.shape["pos"]
        self.near = 2
        self.far = images // CORES // self.near
        self.y = 1
        while (self.y * 2) ** 2 <= self.owners and self.owners % (self.y * 2) == 0:
            self.y *= 2
        self.halves = 2
        self.low = self.owners // self.y // self.halves
        assert images == self.far * self.near * CORES
        assert self.owners == self.halves * self.low * self.y
        steps = list(itertools.product(range(self.near), range(self.low), range(self.y)))
        self.steps = sorted(steps, key=rank(OTHER_ORDER))
        self.own_steps = sorted(steps, key=rank(OWN_ORDER))

    def fit(self, slots, positions, width):
        assert positions == self.owners * self.near and slots == LANES
        self.slots, self.width = slots, width
        self.group = positions // self.halves
        self.blocks = (width + 1) // LANES
        self.main = self.blocks * LANES
        self.padded = self.main + LANES
        self.tail = width + 1 - self.main
        self.tail8 = ceil_to(self.tail, 8)
        self.tail_tiles = ceil_to(self.tail, PACK) // PACK
        self.message = (slots + PACK, self.main)
        assert self.tail_tiles <= self.blocks
        self.row_of = {}
        at = 0
        for i in range(self.blocks):
            for j in range(i + 1, self.blocks):
                self.row_of[(i, j)] = at
                at += LANES
        for i in range(0, self.blocks, 2):
            self.row_of[(i, i)] = at
            at += LANES
        for j in range(self.blocks + 1):
            self.row_of[("tail", j)] = at
            at += self.tail8
        self.row_of["diag"] = at
        self.rows = ceil_to(at + -(-self.blocks // 2), 8 * CORES)
        self.part = self.rows // CORES
        sizes = [self.part // 8 // PIECES + (k < self.part // 8 % PIECES) for k in range(PIECES)]
        ends = [8 * e for e in itertools.accumulate(sizes)]
        self.cuts = [slice(e - 8 * n, e) for e, n in zip(ends, sizes)]

    def moved(self, far=0, near=0, core=0, half=0, low=0, y=0):
        sizes = (self.far, self.near, CORES, self.halves, self.low, self.y)
        shift = (far, near, core, half, low, y)
        pairs = []
        for here in itertools.product(*map(range, sizes)):
            to = [(h + d) % n for h, d, n in zip(here, shift, sizes)]
            index = lambda at: functools.reduce(lambda a, b: a * b[1] + b[0], zip(at, sizes), 0)
            pairs.append((index(here), index(to)))
        return pairs

    def here(self):
        img, pos = lax.axis_index("img"), lax.axis_index("pos")
        return Here(
            near=lax.rem(img // CORES, self.near),
            core=lax.rem(img, CORES),
            half=pos // (self.y * self.low),
            low=lax.rem(pos // self.y, self.low),
            y=lax.rem(pos, self.y),
        )

    def send(self, value, **step):
        if not any(step.values()):
            return value
        return lax.ppermute(value, AXES, self.moved(**step))


def pick(plan, xs, hot, counts_ref, outs, picked, tails, wait):
    slots, _, channels = xs.shape
    block = slots // STEPS
    at = plan.here()
    ones = lax.broadcasted_iota(jnp.int32, (1, plan.padded), 1) == plan.width
    image = lax.broadcasted_iota(jnp.int32, (block * plan.group, 1), 0) // plan.group
    for step in range(STEPS):
        wait(step)
        images = slice(step * block, (step + 1) * block)
        x = xs[images].reshape(block * plan.group, channels)
        got = jnp.dot(x, hot[...], preferred_element_type=jnp.float32)
        got = jnp.where(image < counts_ref[0] - step * block, jnp.where(ones, 1.0, got), 0.0)
        slot = step % 2
        for j in range(plan.blocks + 1):
            picked[slot, j] = got[:, j * LANES : (j + 1) * LANES]
        for k, (out, (dx, dl, dy)) in enumerate(zip(outs, plan.steps)):
            near = lax.rem(at.near + dx, plan.near)
            low = lax.rem(at.low + dl, plan.low)
            y = lax.rem(at.y + dy, plan.y)
            p = (low * plan.y + y) * plan.near + near
            rows = pl.ds(p, block, stride=plan.group)
            for j in range(plan.blocks):
                out[images, j * LANES : (j + 1) * LANES] = picked[slot, j, rows, :].astype(jnp.bfloat16)
            tails[k, images, :] = picked[slot, plan.blocks, rows, :]
    for k, out in enumerate(outs):
        flipped = jnp.transpose(tails[k]).astype(jnp.bfloat16)
        for t in range(plan.tail_tiles):
            out[slots:, t * LANES : (t + 1) * LANES] = flipped[t * PACK : (t + 1) * PACK]
        if plan.tail_tiles < plan.blocks:
            out[slots:, plan.tail_tiles * LANES :] = jnp.zeros(
                (PACK, plan.main - plan.tail_tiles * LANES), jnp.bfloat16
            )


def select_other_kernel(plan, counts_ref, index_hbm, x_hbm, *refs):
    outs, (own, hot), (other, index_ref, picked, tails, sems) = refs[:-7], refs[-7:-5], refs[-5:]
    slots, _, channels = own.shape
    block = slots // STEPS
    half = plan.here().half

    def fetch(flip, step):
        images = pl.ds(step * block, block)
        first = lax.rem(half + flip, plan.halves) * plan.group
        group = pl.ds(pl.multiple_of(first, plan.group), plan.group)
        to = other if flip else own
        return pltpu.make_async_copy(x_hbm.at[images, group, :], to.at[images], sems.at[flip, step])

    fetch_index = pltpu.make_async_copy(index_hbm, index_ref, sems.at[0, STEPS])
    fetch_index.start()
    for flip in (1, 0):
        for step in range(STEPS):
            fetch(flip, step).start()
    fetch_index.wait()
    index = index_ref[...].reshape(1, plan.width)
    rows = lax.broadcasted_iota(jnp.int32, (channels, LANES), 0)
    for j in range(plan.blocks + 1):
        lanes = index[:, j * LANES : min((j + 1) * LANES, plan.width)]
        if lanes.shape[1] < LANES:
            lanes = jnp.concatenate([lanes, jnp.full((1, LANES - lanes.shape[1]), -1, jnp.int32)], axis=1)
        hot[:, j * LANES : (j + 1) * LANES] = jnp.where(rows == lanes, 1.0, 0.0).astype(jnp.bfloat16)
    pick(plan, other, hot, counts_ref, outs, picked, tails, lambda step: fetch(1, step).wait())
    for step in range(STEPS):
        fetch(0, step).wait()


def select_own_kernel(plan, counts_ref, own, hot, *refs):
    outs, (picked, tails) = refs[:-2], refs[-2:]
    pick(plan, own, hot, counts_ref, outs, picked, tails, lambda step: None)


def select(plan, kernel, inputs, kept, scratch, channels):
    count = len(plan.steps)
    vmem, anywhere = pl.BlockSpec(memory_space=pltpu.VMEM), pl.BlockSpec(memory_space=pl.ANY)
    first = bool(kept)
    outs = pl.pallas_call(
        functools.partial(kernel, plan),
        in_specs=[pl.BlockSpec(memory_space=pltpu.SMEM)] + [anywhere if first else vmem] * 2,
        out_specs=[vmem] * (count + len(kept)),
        scratch_shapes=scratch
        + [
            pltpu.VMEM((2, plan.blocks + 1, plan.slots // STEPS * plan.group, LANES), jnp.float32),
            pltpu.VMEM((count, plan.slots, LANES), jnp.float32),
        ]
        + ([pltpu.SemaphoreType.DMA((2, STEPS + 1))] if first else []),
        out_shape=[jax.ShapeDtypeStruct(plan.message, jnp.bfloat16)] * count + kept,
        compiler_params=pltpu.CompilerParams(vmem_limit_bytes=LIMIT << 20),
        cost_estimate=pl.CostEstimate(
            flops=2 * plan.slots * plan.group * channels * plan.padded,
            bytes_accessed=2 * plan.slots * plan.group * (channels + plan.padded),
            transcendentals=0,
        ),
    )(*inputs)
    return dict(zip(plan.steps, outs)), outs[count:]


def select_other(plan, counts, index, features):
    slots, _, channels = features.shape
    half = (slots, plan.group, channels)
    return select(
        plan,
        select_other_kernel,
        (counts, *(pltpu.with_memory_space_constraint(v, pltpu.HBM) for v in (index, features))),
        [
            jax.ShapeDtypeStruct(half, features.dtype),
            jax.ShapeDtypeStruct((channels, plan.padded), jnp.bfloat16),
        ],
        [pltpu.VMEM(half, features.dtype), pltpu.VMEM((plan.width,), jnp.int32)],
        channels,
    )


def select_own(plan, counts, own, hot):
    return select(plan, select_own_kernel, (counts, own, hot), [], [], own.shape[2])[0]


def gram_kernel(plan, *refs):
    ins, (keep, give, out) = refs[:-3], refs[-3:]
    tail8 = plan.tail8
    slots = ins[0].shape[0] - PACK
    rows = jnp.concatenate([r[:slots, :] for r in ins], axis=0)
    tiles = [slice(t * LANES, (t + 1) * LANES) for t in range(plan.tail_tiles)]
    last = jnp.concatenate(
        [jnp.concatenate([r[slots:, t] for t in tiles], axis=0) for r in ins], axis=1
    )
    sub = lax.broadcasted_iota(jnp.int32, (LANES, LANES), 0)
    lane = lax.broadcasted_iota(jnp.int32, (LANES, LANES), 1)

    def put(key, value):
        at = plan.row_of[key]
        out[at : at + value.shape[0], :] = value

    held = None
    contract = (((0,), (0,)), ((), ()))
    for i in range(plan.blocks):
        left = rows[:, i * LANES : (i + 1) * LANES]
        strip = lax.dot_general(left, rows[:, i * LANES :], contract, preferred_element_type=jnp.float32)
        for j in range(i + 1, plan.blocks):
            put((i, j), strip[:, (j - i) * LANES : (j - i + 1) * LANES])
        diag = strip[:, :LANES]
        if i % 2 == 0:
            held = diag
            if i + 1 == plan.blocks:
                put((i, i), held)
        else:
            put((i - 1, i - 1), jnp.where(sub <= lane, held, diag))
            at = plan.row_of["diag"] + i // 2
            out[at : at + 1, :] = jnp.sum(jnp.where(sub == lane, diag, 0.0), axis=0, keepdims=True)
    strip = jnp.dot(last, rows, preferred_element_type=jnp.float32)
    for j in range(plan.blocks):
        put(("tail", j), strip[:tail8, j * LANES : (j + 1) * LANES])
    full = jnp.concatenate([last, jnp.zeros((LANES - last.shape[0], last.shape[1]), last.dtype)], axis=0)
    corner = lax.dot_general(
        last, full, (((1,), (1,)), ((), ())), preferred_element_type=jnp.float32
    )
    put(("tail", plan.blocks), corner[:tail8])
    unused = plan.row_of["diag"] + plan.blocks // 2
    out[unused:, :] = jnp.zeros((plan.rows - unused, LANES), jnp.float32)
    core = plan.here().core
    first = pl.multiple_of(core * plan.part, 8)
    second = pl.multiple_of((CORES - 1 - core) * plan.part, 8)
    keep[...] = out[pl.ds(first, plan.part), :]
    give[...] = out[pl.ds(second, plan.part), :]


def gram(plan, rows):
    images = plan.slots * len(rows)
    part = jax.ShapeDtypeStruct((plan.part, LANES), jnp.float32)
    return pl.pallas_call(
        functools.partial(gram_kernel, plan),
        in_specs=[pl.BlockSpec(memory_space=pltpu.VMEM)] * len(rows),
        out_specs=[pl.BlockSpec(memory_space=pltpu.VMEM)] * 2,
        scratch_shapes=[pltpu.VMEM((plan.rows, LANES), jnp.float32)],
        out_shape=[part, part],
        compiler_params=pltpu.CompilerParams(vmem_limit_bytes=24 << 20),
        cost_estimate=pl.CostEstimate(
            flops=2 * images * plan.main * (plan.main // 2 + 2 * LANES),
            bytes_accessed=2 * images * plan.padded + 4 * plan.rows * LANES,
            transcendentals=0,
        ),
    )(*rows)


def finish_kernel(plan, mine, count, *refs):
    parts, (centre_ref, covar_ref) = refs[:count], refs[-6:-4]
    sums, dense, centre_row, sems = refs[-4:]
    here = plan.here()
    for at, part in enumerate(parts):
        cut = plan.cuts[at % PIECES]
        c = here.core if at < PIECES else CORES - 1 - here.core
        sums[pl.ds(pl.multiple_of(c * plan.part + cut.start, 8), cut.stop - cut.start), :] = part[...]
    nb, tail, width, main = plan.blocks, plan.tail, plan.width, plan.main
    position = here.near if mine else plan.near - 1 - here.near
    sub = lax.broadcasted_iota(jnp.int32, (LANES, LANES), 0)
    lane = lax.broadcasted_iota(jnp.int32, (LANES, LANES), 1)
    rest = width - main

    def get(key, size):
        at = plan.row_of[key]
        return sums[at : at + size, :]

    def tail_row(j):
        at = plan.row_of[("tail", j)] + tail - 1
        return sums[at : at + 1, :]

    def copies(p, strip):
        if strip is None:
            return pltpu.make_async_copy(centre_row.at[0], centre_ref.at[p], sems.at[nb + 1])
        rows = pl.ds(strip * LANES, min(LANES, width - strip * LANES))
        return pltpu.make_async_copy(dense.at[rows], covar_ref.at[rows, p, :], sems.at[strip])

    def send(strip):
        for p in range(plan.near):

            @pl.when(position == p)
            def _():
                copies(p, strip).start()

    total = tail_row(nb)[:, tail - 1 : tail]
    centres = [tail_row(j) / total for j in range(nb + 1)]
    columns = [jnp.transpose(jnp.broadcast_to(c, (LANES, LANES))) for c in centres]
    for j in range(nb):
        centre_row[:, j * LANES : (j + 1) * LANES] = centres[j]
    if rest:
        centre_row[:, main:width] = centres[nb][:, :rest]
    send(None)
    scale = 1.0 / (total - 1.0)

    def covar(sq, i, j):
        rows = sq.shape[0]
        return (sq - total * columns[i][:rows] * centres[j]) * scale

    for i in range(nb):
        at_i = slice(i * LANES, (i + 1) * LANES)
        pair = i - i % 2
        packed = get((pair, pair), LANES)
        flipped = jnp.transpose(packed)
        if i % 2 == 0:
            sq = jnp.where(sub <= lane, packed, flipped) if i + 1 < nb else packed
        else:
            at = plan.row_of["diag"] + i // 2
            sq = jnp.where(sub == lane, sums[at : at + 1, :], jnp.where(sub > lane, packed, flipped))
        dense[at_i, at_i] = covar(sq, i, i) + jnp.where(sub == lane, REG, 0.0)
        for j in range(i + 1, nb):
            at_j = slice(j * LANES, (j + 1) * LANES)
            block = covar(get((i, j), LANES), i, j)
            dense[at_i, at_j] = block
            dense[at_j, at_i] = jnp.transpose(block)
        if rest:
            block = covar(get(("tail", i), plan.tail8), nb, i)
            dense[main:width, at_i] = block[:rest]
            full = jnp.concatenate([block, jnp.zeros((LANES - plan.tail8, LANES), jnp.float32)], axis=0)
            dense[at_i, main:width] = jnp.transpose(full)[:, :rest]
        send(i)
    if rest:
        t8 = plan.tail8
        block = covar(get(("tail", nb), t8), nb, nb) + jnp.where(sub[:t8] == lane[:t8], REG, 0.0)
        dense[main:width, main:width] = block[:rest, :rest]
        send(nb)
    for strip in [None, *range(nb + bool(rest))]:
        copies(0, strip).wait()


def finish(plan, mine, parts, before=()):
    width, nb = plan.width, plan.blocks
    anywhere = pl.BlockSpec(memory_space=pl.ANY)
    count = len(parts)
    return pl.pallas_call(
        functools.partial(finish_kernel, plan, mine, count),
        in_specs=[pl.BlockSpec(memory_space=pltpu.VMEM)] * count + [anywhere] * len(before),
        out_specs=[anywhere] * 2,
        scratch_shapes=[
            pltpu.VMEM((plan.rows, LANES), jnp.float32),
            pltpu.VMEM((width, width), jnp.float32),
            pltpu.VMEM((1, width), jnp.float32),
            pltpu.SemaphoreType.DMA((nb + 2,)),
        ],
        out_shape=[
            jax.ShapeDtypeStruct((plan.near, width), jnp.float32),
            jax.ShapeDtypeStruct((width, plan.near, width), jnp.float32),
        ],
        input_output_aliases={count + i: i for i in range(len(before))},
        compiler_params=pltpu.CompilerParams(vmem_limit_bytes=24 << 20),
        cost_estimate=pl.CostEstimate(
            flops=8 * width * width, bytes_accessed=8 * width * width, transcendentals=0
        ),
        name="finish_mine" if mine else "finish_other",
    )(*parts, *before)


def body(plan, features, channel_index, image_counts):
    plan.fit(features.shape[0], features.shape[1], channel_index.shape[0])

    def exchange(sent, steps):
        got = []
        for step in steps:
            got.append(plan.send(sent[step], near=step[0], low=step[1], y=step[2]))
        return got

    sent_other, (own, hot) = select_other(plan, image_counts, channel_index, features)
    sent_own = select_own(plan, image_counts, own, hot)
    got_other = exchange(sent_other, plan.steps)
    got_own = exchange(sent_own, plan.own_steps)
    keep, give = gram(plan, got_other)
    took = plan.send(give, core=1)
    crossed = []
    for cut in plan.cuts:
        other = keep[cut] + took[cut]
        crossed.append(plan.send(other, half=1))
    keep, give = gram(plan, got_own)
    took = plan.send(give, core=1)
    mine, other = [], []
    for k, cut in enumerate(plan.cuts):
        total = own = keep[cut] + took[cut] + crossed[k]
        for step in range(1, plan.far):
            total = total + plan.send(own, far=step)
        mine.append(total)
        other.append(plan.send(total, near=1))
    for k in range(PIECES):
        mine.append(plan.send(mine[k], core=1))
    for k in range(PIECES):
        other.append(plan.send(other[k], core=1))
    before = finish(plan, True, mine)
    centre, covar = finish(plan, False, other, before)
    return centre, jnp.transpose(covar, (1, 0, 2))


def solution(mesh):
    placed = (P(("img", "pos"), None, None), P(), P(("img", "pos")))
    plan = Plan(mesh)

    def layer(*args):
        return body(plan, *args)

    return jax.shard_map(
        layer,
        mesh=mesh,
        in_specs=placed,
        out_specs=(P("pos", None), P("pos", None, None)),
        check_vma=False,
    )
```

```python
import collections
import functools
import itertools

import jax
import jax.numpy as jnp
from jax import lax
from jax.experimental import pallas as pl
from jax.experimental.pallas import tpu as pltpu
from jax.sharding import PartitionSpec as P


REG = 0.01
LANES = 128
CORES = 2
PACK = 16
PIECES = 2
STEPS = 4
OTHER_PARTS = [1, 3]
OWN_PARTS = [4]
LIMIT = 44
AXES = ("img", "pos")


def ceil_to(n, m):
    return -(-n // m) * m


Here = collections.namedtuple("Here", ["near", "core", "half", "low", "y"])


OTHER_ORDER = ["", "z", "x", "y", "yz", "xz", "xy", "xyz"]
OWN_ORDER = ["", "z", "yz", "xz", "xyz", "x", "xy", "y"]


def rank(order):
    def key(step):
        dx, dl, dy = step
        return order.index("x" * bool(dx) + "y" * bool(dy) + "z" * bool(dl)), step

    return key


class Plan:
    def __init__(self, mesh):
        images, self.owners = mesh.shape["img"], mesh.shape["pos"]
        self.near = 2
        self.far = images // CORES // self.near
        self.y = 1
        while (self.y * 2) ** 2 <= self.owners and self.owners % (self.y * 2) == 0:
            self.y *= 2
        self.halves = 2
        self.low = self.owners // self.y // self.halves
        assert images == self.far * self.near * CORES
        assert self.owners == self.halves * self.low * self.y
        steps = list(itertools.product(range(self.near), range(self.low), range(self.y)))
        self.steps = sorted(steps, key=rank(OTHER_ORDER))
        self.own_steps = sorted(steps, key=rank(OWN_ORDER))

    def fit(self, slots, positions, width):
        assert positions == self.owners * self.near and slots == LANES
        self.slots, self.width = slots, width
        self.group = positions // self.halves
        self.blocks = (width + 1) // LANES
        self.main = self.blocks * LANES
        self.padded = self.main + LANES
        self.tail = width + 1 - self.main
        self.tail8 = ceil_to(self.tail, 8)
        self.tail_tiles = ceil_to(self.tail, PACK) // PACK
        self.message = (slots + PACK, self.main)
        assert self.tail_tiles <= self.blocks
        self.row_of = {}
        at = 0
        for i in range(self.blocks):
            for j in range(i + 1, self.blocks):
                self.row_of[(i, j)] = at
                at += LANES
        for i in range(0, self.blocks, 2):
            self.row_of[(i, i)] = at
            at += LANES
        for j in range(self.blocks + 1):
            self.row_of[("tail", j)] = at
            at += self.tail8
        self.row_of["diag"] = at
        self.rows = ceil_to(at + -(-self.blocks // 2), 8 * CORES)
        self.part = self.rows // CORES
        sizes = [self.part // 8 // PIECES + (k < self.part // 8 % PIECES) for k in range(PIECES)]
        ends = [8 * e for e in itertools.accumulate(sizes)]
        self.cuts = [slice(e - 8 * n, e) for e, n in zip(ends, sizes)]

    def moved(self, far=0, near=0, core=0, half=0, low=0, y=0):
        sizes = (self.far, self.near, CORES, self.halves, self.low, self.y)
        shift = (far, near, core, half, low, y)
        pairs = []
        for here in itertools.product(*map(range, sizes)):
            to = [(h + d) % n for h, d, n in zip(here, shift, sizes)]
            index = lambda at: functools.reduce(lambda a, b: a * b[1] + b[0], zip(at, sizes), 0)
            pairs.append((index(here), index(to)))
        return pairs

    def here(self):
        img, pos = lax.axis_index("img"), lax.axis_index("pos")
        return Here(
            near=lax.rem(img // CORES, self.near),
            core=lax.rem(img, CORES),
            half=pos // (self.y * self.low),
            low=lax.rem(pos // self.y, self.low),
            y=lax.rem(pos, self.y),
        )

    def send(self, value, **step):
        if not any(step.values()):
            return value
        return lax.ppermute(value, AXES, self.moved(**step))


def pick(plan, parts, xs, hot, counts_ref, outs, picked, tails, wait):
    slots, _, channels = xs.shape
    starts = [0, *itertools.accumulate(slots * p // 4 for p in parts)]
    at = plan.here()
    ones = lax.broadcasted_iota(jnp.int32, (1, plan.padded), 1) == plan.width
    for step, (start, stop) in enumerate(zip(starts, starts[1:])):
        wait(step)
        block, images = stop - start, slice(start, stop)
        image = start + lax.broadcasted_iota(jnp.int32, (block * plan.group, 1), 0) // plan.group
        x = xs[images].reshape(block * plan.group, channels)
        got = jnp.dot(x, hot[...], preferred_element_type=jnp.float32)
        got = jnp.where(image < counts_ref[0], jnp.where(ones, 1.0, got), 0.0)
        slot = step % 2
        for j in range(plan.blocks + 1):
            picked[slot, j, : block * plan.group, :] = got[:, j * LANES : (j + 1) * LANES]
        for k, (out, (dx, dl, dy)) in enumerate(zip(outs, plan.steps)):
            near = lax.rem(at.near + dx, plan.near)
            low = lax.rem(at.low + dl, plan.low)
            y = lax.rem(at.y + dy, plan.y)
            p = (low * plan.y + y) * plan.near + near
            rows = pl.ds(p, block, stride=plan.group)
            for j in range(plan.blocks):
                out[images, j * LANES : (j + 1) * LANES] = picked[slot, j, rows, :].astype(jnp.bfloat16)
            tails[k, images, :] = picked[slot, plan.blocks, rows, :]
    for k, out in enumerate(outs):
        flipped = jnp.transpose(tails[k]).astype(jnp.bfloat16)
        for t in range(plan.tail_tiles):
            out[slots:, t * LANES : (t + 1) * LANES] = flipped[t * PACK : (t + 1) * PACK]
        if plan.tail_tiles < plan.blocks:
            out[slots:, plan.tail_tiles * LANES :] = jnp.zeros(
                (PACK, plan.main - plan.tail_tiles * LANES), jnp.bfloat16
            )


def select_other_kernel(plan, counts_ref, index_hbm, x_hbm, *refs):
    outs, (own, hot), (other, index_ref, picked, tails, sems) = refs[:-7], refs[-7:-5], refs[-5:]
    slots, _, channels = own.shape
    block = slots // STEPS
    half = plan.here().half

    def fetch(flip, step):
        images = pl.ds(step * block, block)
        first = lax.rem(half + flip, plan.halves) * plan.group
        group = pl.ds(pl.multiple_of(first, plan.group), plan.group)
        to = other if flip else own
        return pltpu.make_async_copy(x_hbm.at[images, group, :], to.at[images], sems.at[flip, step])

    fetch_index = pltpu.make_async_copy(index_hbm, index_ref, sems.at[0, STEPS])
    fetch_index.start()
    for flip in (1, 0):
        for step in range(STEPS):
            fetch(flip, step).start()
    fetch_index.wait()
    index = index_ref[...].reshape(1, plan.width)
    rows = lax.broadcasted_iota(jnp.int32, (channels, LANES), 0)
    for j in range(plan.blocks + 1):
        lanes = index[:, j * LANES : min((j + 1) * LANES, plan.width)]
        if lanes.shape[1] < LANES:
            lanes = jnp.concatenate([lanes, jnp.full((1, LANES - lanes.shape[1]), -1, jnp.int32)], axis=1)
        hot[:, j * LANES : (j + 1) * LANES] = jnp.where(rows == lanes, 1.0, 0.0).astype(jnp.bfloat16)
    wait = lambda step: [fetch(1, k).wait() for k in range(sum(OTHER_PARTS[:step]), sum(OTHER_PARTS[: step + 1]))]
    pick(plan, OTHER_PARTS, other, hot, counts_ref, outs, picked, tails, wait)
    for step in range(STEPS):
        fetch(0, step).wait()


def select_own_kernel(plan, counts_ref, own, hot, *refs):
    outs, (picked, tails) = refs[:-2], refs[-2:]
    pick(plan, OWN_PARTS, own, hot, counts_ref, outs, picked, tails, lambda step: None)


def select(plan, kernel, inputs, kept, scratch, channels):
    count = len(plan.steps)
    vmem, anywhere = pl.BlockSpec(memory_space=pltpu.VMEM), pl.BlockSpec(memory_space=pl.ANY)
    first = bool(kept)
    outs = pl.pallas_call(
        functools.partial(kernel, plan),
        in_specs=[pl.BlockSpec(memory_space=pltpu.SMEM)] + [anywhere if first else vmem] * 2,
        out_specs=[vmem] * (count + len(kept)),
        scratch_shapes=scratch
        + [
            pltpu.VMEM((2, plan.blocks + 1, plan.slots * plan.group, LANES), jnp.float32),
            pltpu.VMEM((count, plan.slots, LANES), jnp.float32),
        ]
        + ([pltpu.SemaphoreType.DMA((2, STEPS + 1))] if first else []),
        out_shape=[jax.ShapeDtypeStruct(plan.message, jnp.bfloat16)] * count + kept,
        compiler_params=pltpu.CompilerParams(vmem_limit_bytes=LIMIT << 20),
        cost_estimate=pl.CostEstimate(
            flops=2 * plan.slots * plan.group * channels * plan.padded,
            bytes_accessed=2 * plan.slots * plan.group * (channels + plan.padded),
            transcendentals=0,
        ),
    )(*inputs)
    return dict(zip(plan.steps, outs)), outs[count:]


def select_other(plan, counts, index, features):
    slots, _, channels = features.shape
    half = (slots, plan.group, channels)
    return select(
        plan,
        select_other_kernel,
        (counts, *(pltpu.with_memory_space_constraint(v, pltpu.HBM) for v in (index, features))),
        [
            jax.ShapeDtypeStruct(half, features.dtype),
            jax.ShapeDtypeStruct((channels, plan.padded), jnp.bfloat16),
        ],
        [pltpu.VMEM(half, features.dtype), pltpu.VMEM((plan.width,), jnp.int32)],
        channels,
    )


def select_own(plan, counts, own, hot):
    return select(plan, select_own_kernel, (counts, own, hot), [], [], own.shape[2])[0]


def gram_kernel(plan, *refs):
    ins, (keep, give, out) = refs[:-3], refs[-3:]
    tail8 = plan.tail8
    slots = ins[0].shape[0] - PACK
    rows = jnp.concatenate([r[:slots, :] for r in ins], axis=0)
    tiles = [slice(t * LANES, (t + 1) * LANES) for t in range(plan.tail_tiles)]
    last = jnp.concatenate(
        [jnp.concatenate([r[slots:, t] for t in tiles], axis=0) for r in ins], axis=1
    )
    sub = lax.broadcasted_iota(jnp.int32, (LANES, LANES), 0)
    lane = lax.broadcasted_iota(jnp.int32, (LANES, LANES), 1)

    def put(key, value):
        at = plan.row_of[key]
        out[at : at + value.shape[0], :] = value

    held = None
    contract = (((0,), (0,)), ((), ()))
    for i in range(plan.blocks):
        left = rows[:, i * LANES : (i + 1) * LANES]
        strip = lax.dot_general(left, rows[:, i * LANES :], contract, preferred_element_type=jnp.float32)
        for j in range(i + 1, plan.blocks):
            put((i, j), strip[:, (j - i) * LANES : (j - i + 1) * LANES])
        diag = strip[:, :LANES]
        if i % 2 == 0:
            held = diag
            if i + 1 == plan.blocks:
                put((i, i), held)
        else:
            put((i - 1, i - 1), jnp.where(sub <= lane, held, diag))
            at = plan.row_of["diag"] + i // 2
            out[at : at + 1, :] = jnp.sum(jnp.where(sub == lane, diag, 0.0), axis=0, keepdims=True)
    strip = jnp.dot(last, rows, preferred_element_type=jnp.float32)
    for j in range(plan.blocks):
        put(("tail", j), strip[:tail8, j * LANES : (j + 1) * LANES])
    full = jnp.concatenate([last, jnp.zeros((LANES - last.shape[0], last.shape[1]), last.dtype)], axis=0)
    corner = lax.dot_general(
        last, full, (((1,), (1,)), ((), ())), preferred_element_type=jnp.float32
    )
    put(("tail", plan.blocks), corner[:tail8])
    unused = plan.row_of["diag"] + plan.blocks // 2
    out[unused:, :] = jnp.zeros((plan.rows - unused, LANES), jnp.float32)
    core = plan.here().core
    first = pl.multiple_of(core * plan.part, 8)
    second = pl.multiple_of((CORES - 1 - core) * plan.part, 8)
    keep[...] = out[pl.ds(first, plan.part), :]
    give[...] = out[pl.ds(second, plan.part), :]


def gram(plan, rows):
    images = plan.slots * len(rows)
    part = jax.ShapeDtypeStruct((plan.part, LANES), jnp.float32)
    return pl.pallas_call(
        functools.partial(gram_kernel, plan),
        in_specs=[pl.BlockSpec(memory_space=pltpu.VMEM)] * len(rows),
        out_specs=[pl.BlockSpec(memory_space=pltpu.VMEM)] * 2,
        scratch_shapes=[pltpu.VMEM((plan.rows, LANES), jnp.float32)],
        out_shape=[part, part],
        compiler_params=pltpu.CompilerParams(vmem_limit_bytes=24 << 20),
        cost_estimate=pl.CostEstimate(
            flops=2 * images * plan.main * (plan.main // 2 + 2 * LANES),
            bytes_accessed=2 * images * plan.padded + 4 * plan.rows * LANES,
            transcendentals=0,
        ),
    )(*rows)


def finish_kernel(plan, mine, count, *refs):
    parts, (centre_ref, covar_ref) = refs[:count], refs[-6:-4]
    sums, dense, centre_row, sems = refs[-4:]
    here = plan.here()
    for at, part in enumerate(parts):
        cut = plan.cuts[at % PIECES]
        c = here.core if at < PIECES else CORES - 1 - here.core
        sums[pl.ds(pl.multiple_of(c * plan.part + cut.start, 8), cut.stop - cut.start), :] = part[...]
    nb, tail, width, main = plan.blocks, plan.tail, plan.width, plan.main
    position = here.near if mine else plan.near - 1 - here.near
    sub = lax.broadcasted_iota(jnp.int32, (LANES, LANES), 0)
    lane = lax.broadcasted_iota(jnp.int32, (LANES, LANES), 1)
    rest = width - main

    def get(key, size):
        at = plan.row_of[key]
        return sums[at : at + size, :]

    def tail_row(j):
        at = plan.row_of[("tail", j)] + tail - 1
        return sums[at : at + 1, :]

    def copies(p, strip):
        if strip is None:
            return pltpu.make_async_copy(centre_row.at[0], centre_ref.at[p], sems.at[nb + 1])
        rows = pl.ds(strip * LANES, min(LANES, width - strip * LANES))
        return pltpu.make_async_copy(dense.at[rows], covar_ref.at[rows, p, :], sems.at[strip])

    def send(strip):
        for p in range(plan.near):

            @pl.when(position == p)
            def _():
                copies(p, strip).start()

    total = tail_row(nb)[:, tail - 1 : tail]
    centres = [tail_row(j) / total for j in range(nb + 1)]
    columns = [jnp.transpose(jnp.broadcast_to(c, (LANES, LANES))) for c in centres]
    for j in range(nb):
        centre_row[:, j * LANES : (j + 1) * LANES] = centres[j]
    if rest:
        centre_row[:, main:width] = centres[nb][:, :rest]
    send(None)
    scale = 1.0 / (total - 1.0)

    def covar(sq, i, j):
        rows = sq.shape[0]
        return (sq - total * columns[i][:rows] * centres[j]) * scale

    for i in range(nb):
        at_i = slice(i * LANES, (i + 1) * LANES)
        pair = i - i % 2
        packed = get((pair, pair), LANES)
        flipped = jnp.transpose(packed)
        if i % 2 == 0:
            sq = jnp.where(sub <= lane, packed, flipped) if i + 1 < nb else packed
        else:
            at = plan.row_of["diag"] + i // 2
            sq = jnp.where(sub == lane, sums[at : at + 1, :], jnp.where(sub > lane, packed, flipped))
        dense[at_i, at_i] = covar(sq, i, i) + jnp.where(sub == lane, REG, 0.0)
        for j in range(i + 1, nb):
            at_j = slice(j * LANES, (j + 1) * LANES)
            block = covar(get((i, j), LANES), i, j)
            dense[at_i, at_j] = block
            dense[at_j, at_i] = jnp.transpose(block)
        if rest:
            block = covar(get(("tail", i), plan.tail8), nb, i)
            dense[main:width, at_i] = block[:rest]
            full = jnp.concatenate([block, jnp.zeros((LANES - plan.tail8, LANES), jnp.float32)], axis=0)
            dense[at_i, main:width] = jnp.transpose(full)[:, :rest]
        send(i)
    if rest:
        t8 = plan.tail8
        block = covar(get(("tail", nb), t8), nb, nb) + jnp.where(sub[:t8] == lane[:t8], REG, 0.0)
        dense[main:width, main:width] = block[:rest, :rest]
        send(nb)
    for strip in [None, *range(nb + bool(rest))]:
        copies(0, strip).wait()


def finish(plan, mine, parts, before=()):
    width, nb = plan.width, plan.blocks
    anywhere = pl.BlockSpec(memory_space=pl.ANY)
    count = len(parts)
    return pl.pallas_call(
        functools.partial(finish_kernel, plan, mine, count),
        in_specs=[pl.BlockSpec(memory_space=pltpu.VMEM)] * count + [anywhere] * len(before),
        out_specs=[anywhere] * 2,
        scratch_shapes=[
            pltpu.VMEM((plan.rows, LANES), jnp.float32),
            pltpu.VMEM((width, width), jnp.float32),
            pltpu.VMEM((1, width), jnp.float32),
            pltpu.SemaphoreType.DMA((nb + 2,)),
        ],
        out_shape=[
            jax.ShapeDtypeStruct((plan.near, width), jnp.float32),
            jax.ShapeDtypeStruct((width, plan.near, width), jnp.float32),
        ],
        input_output_aliases={count + i: i for i in range(len(before))},
        compiler_params=pltpu.CompilerParams(vmem_limit_bytes=24 << 20),
        cost_estimate=pl.CostEstimate(
            flops=8 * width * width, bytes_accessed=8 * width * width, transcendentals=0
        ),
        name="finish_mine" if mine else "finish_other",
    )(*parts, *before)


def body(plan, features, channel_index, image_counts):
    plan.fit(features.shape[0], features.shape[1], channel_index.shape[0])

    def exchange(sent, steps):
        got = []
        for step in steps:
            got.append(plan.send(sent[step], near=step[0], low=step[1], y=step[2]))
        return got

    sent_other, (own, hot) = select_other(plan, image_counts, channel_index, features)
    sent_own = select_own(plan, image_counts, own, hot)
    got_other = exchange(sent_other, plan.steps)
    got_own = exchange(sent_own, plan.own_steps)
    keep, give = gram(plan, got_other)
    took = plan.send(give, core=1)
    crossed = []
    for cut in plan.cuts:
        other = keep[cut] + took[cut]
        crossed.append(plan.send(other, half=1))
    keep, give = gram(plan, got_own)
    took = plan.send(give, core=1)
    mine, other = [], []
    for k, cut in enumerate(plan.cuts):
        total = own = keep[cut] + took[cut] + crossed[k]
        for step in range(1, plan.far):
            total = total + plan.send(own, far=step)
        mine.append(total)
        other.append(plan.send(total, near=1))
    for k in range(PIECES):
        mine.append(plan.send(mine[k], core=1))
    for k in range(PIECES):
        other.append(plan.send(other[k], core=1))
    before = finish(plan, True, mine)
    centre, covar = finish(plan, False, other, before)
    return centre, jnp.transpose(covar, (1, 0, 2))


def solution(mesh):
    placed = (P(("img", "pos"), None, None), P(), P(("img", "pos")))
    plan = Plan(mesh)

    def layer(*args):
        return body(plan, *args)

    return jax.shard_map(
        layer,
        mesh=mesh,
        in_specs=placed,
        out_specs=(P("pos", None), P("pos", None, None)),
        check_vma=False,
    )
```
